512 devices in a mesh: mode: 32 (over z_lo, y), tile: 16 (over z_hi, x, core).
Axes of the slice: x: 4, y: 4, z: 16 (z_hi: 2, z_lo: 8; z = z_hi * 8 + z_lo), core: 2. Of those that a mesh axis runs over, the one named last changes fastest.
Arguments:
- magnetic: float32 [128, 6, 32, 2048], P('mode', None, None, 'tile'), may hold values from -6 to 6
- velocity_stack: float32 [32, 9, 32, 2048], P('mode', None, None, 'tile'), may hold values from -6 to 6
- wavenumber: int32 [128], P('mode'), may hold values from -64 to 63, as said below
- velocity_owner: int32 [1], replicated, may hold values from 0 to 31
Outputs:
- evolved: float32 [128, 6, 32, 2048], P('mode', None, None, 'tile')
The draws below stay inside these ranges and needn't reach their ends.
Inputs may be any that keep to these rules, and one draw needn't show every extreme that they name: Slot k holds wavenumber ((k + s) mod 128) - 64 for one whole number s of the draw.
All inputs are finite; a program needn't handle non-finite values.
Results may differ from the reference program's by a relative error of at most 0.0003.
Values sent between devices are 32-bit elements; how exact they have to be, the bound alone decides.
A program may use at most 64 MiB of HBM per device.

```python
import jax
import jax.numpy as jnp
from jax import lax

MODES = 128
ZW = 32
NR = 2048
STEPS = 2
N_MODE = 32


def draw_wavenumber(key, part):
    offset = jax.random.randint(key, (), 0, MODES)
    slots = jnp.arange(MODES, dtype=jnp.int32)
    return ((slots + offset) % MODES - MODES // 2).astype(jnp.int32)


def levels(key, dims, shards, least, top_value):
    factor_of, own = 1.0, jax.random.fold_in(key, 6)
    for position, shards_of in shards:
        heights = jnp.exp(jax.random.uniform(jax.random.fold_in(own, position), (shards_of,), jnp.float32, least / len(shards), top_value / len(shards)))
        factor_of = factor_of * jnp.repeat(heights, dims[position] // shards_of).reshape([-1 if axis == position else 1 for axis in range(len(dims))])
    return factor_of


def noise(stream_key, shape, scale, reach, cuts=(), held_as=jnp.bfloat16):
    drawn = jax.random.normal(stream_key, shape, jnp.float32) * scale
    if len(cuts) > 0:
        drawn = levels(stream_key, shape, cuts, -0.22, 0.18) * drawn
    return jnp.clip(drawn, min=-reach, max=reach).astype(held_as)


def setup_inputs(seed: int = 0) -> dict:
    streams_of = jax.random.split(jax.random.key(seed), 5)
    magnetic = noise(streams_of[0], (MODES, 6, ZW, NR), 1.0, 6.0, ((0, 32), (3, 16)), jnp.float32)
    velocity_stack = noise(streams_of[1], (N_MODE, 9, ZW, NR), 1.0, 6.0, ((0, 32), (3, 16)), jnp.float32)
    wavenumber = draw_wavenumber(jax.random.fold_in(streams_of[4], 71), 0)
    velocity_owner = jax.random.randint(streams_of[3], (1,), 0, N_MODE).astype(jnp.int32)
    return dict(magnetic=magnetic, velocity_stack=velocity_stack, wavenumber=wavenumber, velocity_owner=velocity_owner)


diffusivity = 0.5
time_step = 0.2
inner_radius = 32.0


def complex_product(left_pair, right_pair):
    return (left_pair[0] * right_pair[0] - left_pair[1] * right_pair[1],
            left_pair[0] * right_pair[1] + left_pair[1] * right_pair[0])


def subtract_pair(left_pair, right_pair):
    return (left_pair[0] - right_pair[0], left_pair[1] - right_pair[1])


def components(values):
    return [(values[..., 2 * component, :, :], values[..., 2 * component + 1, :, :]) for component in range(3)]


def cross_product(left_vec, right_vec):
    radial_out = subtract_pair(complex_product(left_vec[1], right_vec[2]), complex_product(left_vec[2], right_vec[1]))
    azimuth_out = subtract_pair(complex_product(left_vec[2], right_vec[0]), complex_product(left_vec[0], right_vec[2]))
    axial_out = subtract_pair(complex_product(left_vec[0], right_vec[1]), complex_product(left_vec[1], right_vec[0]))
    return [radial_out, azimuth_out, axial_out]


def electromotive(velocity, lower_mode, centre, upper_mode):
    nothing = jnp.zeros_like(velocity[0])
    steady = [(velocity[0], nothing), (velocity[1], nothing), (velocity[2], nothing)]
    swirling = [(velocity[3], velocity[4]), (velocity[5], velocity[6]), (velocity[7], velocity[8])]
    mirror = [(pair[0], -pair[1]) for pair in swirling]
    first = cross_product(steady, components(centre))
    second = cross_product(swirling, components(lower_mode))
    third = cross_product(mirror, components(upper_mode))
    pieces = []
    for component in range(3):
        for part_index in range(2):
            pieces.append(first[component][part_index] + second[component][part_index] + third[component][part_index])
    return jnp.stack(pieces, axis=-3)


def interior(values):
    return values[..., 1:-1]


def pad_axial(values):
    return jnp.pad(values, [(0, 0)] * (values.ndim - 2) + [(1, 1), (0, 0)])


def along_axial(values):
    padded = pad_axial(values)
    return 0.5 * (padded[..., 2:, :] - padded[..., :-2, :])


def along_radial(values):
    return 0.5 * (values[..., 2:] - values[..., :-2])


def laplace(values, radius):
    centre = interior(values)
    padded = pad_axial(centre)
    return (values[..., 2:] + values[..., :-2] + padded[..., 2:, :] + padded[..., :-2, :]
            - 4.0 * centre + along_radial(values) / radius)


def radial_flux(values, radius):
    return 0.5 * ((radius + 1.0) * values[..., 2:] - (radius - 1.0) * values[..., :-2]) / radius


def rates(wide_field, wide_emf, waves, radius):
    field_r, field_p, field_z = components(wide_field)
    emf_r, emf_p, emf_z = components(wide_emf)
    wave_over = waves / radius
    decay_rate = (waves * waves + 1.0) / (radius * radius)
    coupling = 2.0 * waves / (radius * radius)
    axial_decay = waves * waves / (radius * radius)
    r_real = (-wave_over * interior(emf_z[1]) - along_axial(interior(emf_p[0]))
              + diffusivity * (laplace(field_r[0], radius) - decay_rate * interior(field_r[0]) + coupling * interior(field_p[1])))
    r_imag = (wave_over * interior(emf_z[0]) - along_axial(interior(emf_p[1]))
              + diffusivity * (laplace(field_r[1], radius) - decay_rate * interior(field_r[1]) - coupling * interior(field_p[0])))
    p_real = (along_axial(interior(emf_r[0])) - along_radial(emf_z[0])
              + diffusivity * (laplace(field_p[0], radius) - decay_rate * interior(field_p[0]) - coupling * interior(field_r[1])))
    p_imag = (along_axial(interior(emf_r[1])) - along_radial(emf_z[1])
              + diffusivity * (laplace(field_p[1], radius) - decay_rate * interior(field_p[1]) + coupling * interior(field_r[0])))
    z_real = (radial_flux(emf_p[0], radius) + wave_over * interior(emf_r[1])
              + diffusivity * (laplace(field_z[0], radius) - axial_decay * interior(field_z[0])))
    z_imag = (radial_flux(emf_p[1], radius) - wave_over * interior(emf_r[0])
              + diffusivity * (laplace(field_z[1], radius) - axial_decay * interior(field_z[1])))
    return jnp.stack([r_real, r_imag, p_real, p_imag, z_real, z_imag], axis=-3)


def evaluate(state, velocity, wavenumber, radius):
    modes_total = state.shape[0]

    def one_mode(slot):
        below = lax.dynamic_index_in_dim(state, ((slot - 1) % modes_total).astype(jnp.int32), 0, keepdims=False)
        centre = lax.dynamic_index_in_dim(state, slot, 0, keepdims=False)
        above = lax.dynamic_index_in_dim(state, ((slot + 1) % modes_total).astype(jnp.int32), 0, keepdims=False)
        emf = electromotive(velocity, below, centre, above)
        widths = ((0, 0), (0, 0), (1, 1))
        waves = lax.dynamic_index_in_dim(wavenumber, slot, 0, keepdims=False).astype(jnp.float32)
        return rates(jnp.pad(centre, widths), jnp.pad(emf, widths), waves, radius)

    return lax.map(one_mode, jnp.arange(modes_total, dtype=jnp.int32))


def reference(magnetic, velocity_stack, wavenumber, velocity_owner):
    velocity = lax.dynamic_index_in_dim(velocity_stack, velocity_owner[0].astype(jnp.int32), 0, keepdims=False)
    radius = inner_radius + jnp.arange(magnetic.shape[3], dtype=jnp.int32).astype(jnp.float32) + 0.5
    state = magnetic
    for step_index in range(STEPS):
        first = evaluate(state, velocity, wavenumber, radius)
        trial = state + time_step * first
        second = evaluate(trial, velocity, wavenumber, radius)
        state = state + (0.5 * time_step) * (first + second)
    return state
```

```python
import functools

import jax
import jax.numpy as jnp
from jax import lax
from jax.experimental import pallas as pl
from jax.experimental.pallas import tpu as pltpu
from jax.sharding import PartitionSpec as P

MESH = pl.DeviceIdType.MESH
TIME_STEP = 0.2
INNER = 32.0
F32 = jnp.float32


def kernel(n_tile, wave_ref, owner_ref, mag, vel, out, S, T, Vin, M, Ry, Q, Rz, R8, V, U, W, coef, pack, fromL, fromR,
           lsem, ysend, yrecv, zsend, zrecv, z8send, z8recv, gsend, grecv, g8send, g8recv, asend, arecv,
           msend, mrecv, tsend, trecv):
    mode = lax.axis_index("mode")
    tile = lax.axis_index("tile")
    zc = mode // 4
    yc = mode % 4

    load_v = pltpu.make_async_copy(vel.at[0], Vin, lsem.at[0])
    load_v.start()
    load_s = pltpu.make_async_copy(mag, S.at[pl.ds(4, 4)], lsem.at[1])
    load_s.start()

    mode_up = (mode + 1) % 32
    mode_dn = (mode + 31) % 32
    tile_up = (tile + 1) % n_tile
    tile_dn = (tile + n_tile - 1) % n_tile
    ypeer = [zc * 4 + (yc + d) % 4 for d in (1, 2, 3)]
    zpos = [(zc + d) % 8 for d in range(1, 8)]
    zpeer = [p * 4 + yc for p in zpos]

    barrier = pltpu.get_barrier_semaphore()
    greet = [(m, tile) for m in ypeer + zpeer + [mode_up, mode_dn]] + [(mode, tile_up), (mode, tile_dn)]
    for where in greet:
        pl.semaphore_signal(barrier, inc=1, device_id=where, device_id_type=MESH)

    lane = lax.broadcasted_iota(jnp.int32, (8, 128), 1)
    radius = INNER + (tile * 128 + lane).astype(F32) + 0.5
    inv = 1.0 / radius
    before = radius - 1.0
    after = radius + 1.0
    coef[0] = 0.5 + 0.25 / before
    coef[1] = 0.5 - 0.25 / after
    coef[2] = 0.5 * radius / before
    coef[3] = 0.5 * radius / after
    coef[4] = inv
    coef[5] = 1.0 / (radius * radius)
    zero = jnp.zeros((8, 128), F32)
    for c in range(6):
        for edge in (0, 40):
            U[c, edge:edge + 8, :] = zero
            if c < 4:
                W[c, edge:edge + 8, :] = zero

    load_v.wait()
    mine = owner_ref[0] == mode
    M[...] = jnp.where(mine, Vin[...], 0.0)
    pl.semaphore_wait(barrier, len(greet))

    ycopies = []
    for i, d in enumerate((1, 2, 3)):
        rows = pl.ds(pl.multiple_of(((yc + d) % 4) * 8, 8), 8)
        ycopies.append(pltpu.make_async_remote_copy(
            M.at[:, rows, :], Ry.at[i], ysend.at[i], yrecv.at[i], device_id=(ypeer[i], tile), device_id_type=MESH))
    for copy in ycopies:
        copy.start()
    mcopies = []
    for i in range(4):
        mcopies.append(pltpu.make_async_remote_copy(
            mag.at[3 - i], S.at[3 - i], msend.at[2 * i], mrecv.at[2 * i], device_id=(mode_up, tile), device_id_type=MESH))
        mcopies.append(pltpu.make_async_remote_copy(
            mag.at[i], S.at[8 + i], msend.at[2 * i + 1], mrecv.at[2 * i + 1], device_id=(mode_dn, tile), device_id_type=MESH))
    own = pl.ds(pl.multiple_of(yc * 8, 8), 8)
    for copy in ycopies:
        copy.wait_recv()
    Q[...] = M[:, own, :] + Ry[0] + Ry[1] + Ry[2]

    zcopies, z8copies = [], []
    for i in range(7):
        where = (zpeer[i], tile)
        zcopies.append(pltpu.make_async_remote_copy(
            Q.at[zpos[i]], Rz.at[i], zsend.at[i], zrecv.at[i], device_id=where, device_id_type=MESH))
        z8copies.append(pltpu.make_async_remote_copy(
            Q.at[8], R8.at[i], z8send.at[i], z8recv.at[i], device_id=where, device_id_type=MESH))
    for i in range(7):
        zcopies[i].start()

        @pl.when(zpos[i] == 4)
        def _(i=i):
            z8copies[i].start()

    for copy in mcopies:
        copy.start()
    total = Q[zc]
    for i in range(7):
        zcopies[i].wait_recv()
        total = total + Rz[i]
    V[zc, own, :] = total

    gcopies, g8copies = [], []
    for i in range(7):
        where = (zpeer[i], tile)
        gcopies.append(pltpu.make_async_remote_copy(
            V.at[zc, own, :], V.at[zc, own, :], gsend.at[i], grecv.at[i], device_id=where, device_id_type=MESH))
        g8copies.append(pltpu.make_async_remote_copy(
            V.at[8, own, :], V.at[8, own, :], g8send.at[i], g8recv.at[0], device_id=where, device_id_type=MESH))
    for copy in gcopies:
        copy.start()

    @pl.when(zc == 4)
    def _():
        last = Q[8]
        for i in range(7):
            z8copies[i].wait_recv()
            last = last + R8[i]
        V[8, own, :] = last
        for i in range(7):
            g8copies[i].start()

    for copy in gcopies:
        copy.wait_recv()

    @pl.when(zc != 4)
    def _():
        g8copies[0].wait_recv()

    acopies = []
    for i in range(3):
        acopies.append(pltpu.make_async_remote_copy(
            V.at[:, own, :], V.at[:, own, :], asend.at[i], arecv.at[i], device_id=(ypeer[i], tile), device_id_type=MESH))
    for copy in acopies:
        copy.start()

    load_s.wait()
    for copy in mcopies:
        copy.wait_recv()
    for copy in acopies:
        copy.wait_recv()

    first_wave = wave_ref[0] + 64
    pairs = lane // 2
    edges = (lane == 0) | (lane == 127)
    odd = (lane % 2) == 1

    def half_pass(cur, slot, base, target, where_to, step, blend, acc, index):
        m = (((first_wave + (slot - 4) + 128) & 127) - 64).astype(F32)
        apm, amp, flp, flm, inv, inv2 = (coef[i] for i in range(6))
        w = m * inv
        dec = 2.0 + (0.5 * (m * m + 1.0)) * inv2
        decz = 2.0 + (0.5 * (m * m)) * inv2
        cpl = m * inv2
        for zt in range(4):
            rows = slice(8 * zt, 8 * zt + 8)
            put = slice(8 + 8 * zt, 16 + 8 * zt)
            v = [V[f, rows, :] for f in range(9)]
            b = [cur[slot, c, rows, :] for c in range(6)]
            lo = [cur[slot - 1, c, rows, :] for c in range(6)]
            up = [cur[slot + 1, c, rows, :] for c in range(6)]
            sums = [lo[c] + up[c] for c in range(6)]
            swap = [None] * 6
            for k in range(3):
                swap[2 * k] = up[2 * k + 1] - lo[2 * k + 1]
                swap[2 * k + 1] = lo[2 * k] - up[2 * k]
            e = []
            for k in range(3):
                s, t = (k + 1) % 3, (k + 2) % 3
                for q in range(2):
                    i, j = 2 * t + q, 2 * s + q
                    e.append((v[s] * b[i] - v[t] * b[j]) + (v[3 + 2 * s] * sums[i] + v[4 + 2 * s] * swap[i])
                             - (v[3 + 2 * t] * sums[j] + v[4 + 2 * t] * swap[j]))
            local = [
                cpl * b[3] - w * e[5] - dec * b[0],
                w * e[4] - cpl * b[2] - dec * b[1],
                -(dec * b[2] + cpl * b[1]),
                cpl * b[0] - dec * b[3],
                w * e[1] - decz * b[4],
                -(w * e[0] + decz * b[5]),
            ]
            half_b = [0.5 * b[c] for c in range(6)]
            half_e = [0.5 * e[c] for c in range(6)]
            for q in range(2):
                U[q, put, :] = half_b[q] - half_e[2 + q]
                W[q, put, :] = half_b[q] + half_e[2 + q]
                U[2 + q, put, :] = half_b[2 + q] + half_e[q]
                W[2 + q, put, :] = half_b[2 + q] - half_e[q]
                U[4 + q, put, :] = half_b[4 + q]
            for c in range(6):
                right, left = apm * b[c], amp * b[c]
                if c in (2, 3):
                    right = right - half_e[c + 2]
                    left = left + half_e[c + 2]
                elif c >= 4:
                    right = right + flp * e[c - 2]
                    left = left - flm * e[c - 2]
                i = index + 4 * c + zt
                both = pltpu.roll(jnp.where(lane == 0, right, left), 2 * i + 1, 1)
                acc = jnp.where(pairs == i, both, acc)
                partial = local[c] + pltpu.roll(right, 127, 1) + pltpu.roll(left, 1, 1)
                start = base[slot, c, rows, :]
                if blend:
                    start = 0.5 * start + 0.5 * b[c]
                target[where_to, c, rows, :] = start + step * partial
        for c in range(6):
            low = U if c >= 4 else W
            for zt in range(4):
                rows = slice(8 * zt, 8 * zt + 8)
                moved = U[c, 9 + 8 * zt:17 + 8 * zt, :] + low[c, 7 + 8 * zt:15 + 8 * zt, :]
                target[where_to, c, rows, :] = target[where_to, c, rows, :] + step * moved
        return acc

    tcopies = []
    for e in range(4):
        lowest, count = e + 1, 5 - e
        cur, base = (S, S) if e % 2 == 0 else (T, S)
        target = T if e % 2 == 0 else S
        shift = 0
        if e == 3:
            target, shift = out, 4
        step = TIME_STEP if e % 2 == 0 else 0.5 * TIME_STEP

        @pl.loop(0, count)
        def _(p, cur=cur, base=base, target=target, shift=shift, step=step, lowest=lowest, e=e):
            acc = jnp.zeros((8, 128), F32)
            for k in range(2):
                slot = lowest + 2 * p + k
                acc = half_pass(cur, slot, base, target, slot - shift, step, e % 2 == 1, acc, 24 * k)
            pack[e, p] = acc

        some = pl.ds(0, count)
        right = pltpu.make_async_remote_copy(
            pack.at[e, some], fromL.at[e, some], tsend.at[2 * e], trecv.at[2 * e],
            device_id=(mode, tile_up), device_id_type=MESH)
        left = pltpu.make_async_remote_copy(
            pack.at[e, some], fromR.at[e, some], tsend.at[2 * e + 1], trecv.at[2 * e + 1],
            device_id=(mode, tile_dn), device_id_type=MESH)
        right.start()
        left.start()
        tcopies += [right, left]
        right.wait_recv()
        left.wait_recv()

        @pl.loop(0, count)
        def _(p, target=target, shift=shift, step=step, lowest=lowest, e=e):
            here = pack[e, p]
            on_right = jnp.where(tile == n_tile - 1, 0.0, fromR[e, p]) - here
            on_left = jnp.where(tile == 0, 0.0, fromL[e, p]) - here
            fix = step * jnp.where(odd, on_right, pltpu.roll(on_left, 2, 1))
            for k in range(2):
                to = lowest + 2 * p + k - shift
                for c in range(6):
                    for zt in range(4):
                        i = 24 * k + 4 * c + zt
                        rows = slice(8 * zt, 8 * zt + 8)
                        add = jnp.where(edges, pltpu.roll(fix, 126 - 2 * i, 1), 0.0)
                        target[to, c, rows, :] = target[to, c, rows, :] + add

    for copy in ycopies + mcopies + zcopies + gcopies + acopies + tcopies:
        copy.wait_send()
    for i in range(7):
        @pl.when(zpos[i] == 4)
        def _(i=i):
            z8copies[i].wait_send()

    @pl.when(zc == 4)
    def _():
        for i in range(7):
            g8copies[i].wait_send()


def body(n_tile, magnetic, velocity_stack, wavenumber, velocity_owner):
    vmem = pl.BlockSpec(memory_space=pltpu.VMEM)
    smem = pl.BlockSpec(memory_space=pltpu.SMEM)
    anyw = pl.BlockSpec(memory_space=pl.ANY)
    dma = pltpu.SemaphoreType.DMA
    block = pltpu.VMEM((12, 6, 32, 128), F32)
    return pl.pallas_call(
        functools.partial(kernel, n_tile),
        out_shape=jax.ShapeDtypeStruct((4, 6, 32, 128), F32),
        in_specs=[smem, smem, anyw, anyw],
        out_specs=vmem,
        scratch_shapes=[
            block, block,
            pltpu.VMEM((9, 32, 128), F32), pltpu.VMEM((9, 32, 128), F32),
            pltpu.VMEM((3, 9, 8, 128), F32), pltpu.VMEM((9, 8, 128), F32),
            pltpu.VMEM((7, 8, 128), F32), pltpu.VMEM((7, 8, 128), F32),
            pltpu.VMEM((9, 32, 128), F32),
            pltpu.VMEM((6, 48, 128), F32), pltpu.VMEM((4, 48, 128), F32),
            pltpu.VMEM((6, 8, 128), F32),
            pltpu.VMEM((4, 5, 8, 128), F32), pltpu.VMEM((4, 5, 8, 128), F32), pltpu.VMEM((4, 5, 8, 128), F32),
            dma((2,)), dma((3,)), dma((3,)), dma((7,)), dma((7,)), dma((7,)), dma((7,)),
            dma((7,)), dma((7,)), dma((7,)), dma((1,)), dma((3,)), dma((3,)),
            dma((8,)), dma((8,)), dma((8,)), dma((8,)),
        ],
        compiler_params=pltpu.CompilerParams(collective_id=0, has_side_effects=True, vmem_limit_bytes=32 << 20),
    )(wavenumber, velocity_owner, magnetic, velocity_stack)


def solution(mesh):
    placed = (P("mode", None, None, "tile"), P("mode", None, None, "tile"), P("mode"), P())
    return jax.shard_map(
        functools.partial(body, mesh.shape["tile"]), mesh=mesh, in_specs=placed,
        out_specs=P("mode", None, None, "tile"), check_vma=False,
    )
```

```python
import functools

import jax
import jax.numpy as jnp
from jax import lax
from jax.experimental import pallas as pl
from jax.experimental.pallas import tpu as pltpu
from jax.sharding import PartitionSpec as P

MESH = pl.DeviceIdType.MESH
TIME_STEP = 0.2
INNER = 32.0
F32 = jnp.float32


def radius_rows(radius):
    before, after = radius - 1.0, radius + 1.0
    return [0.5 + 0.25 / before, 0.5 - 0.25 / after, 0.5 * radius / before, 0.5 * radius / after,
            1.0 / radius, 1.0 / (radius * radius)]


def wave_rows(m, rows):
    inv, inv2 = rows[4], rows[5]
    return m * inv, 2.0 + (0.5 * (m * m + 1.0)) * inv2, 2.0 + (0.5 * (m * m)) * inv2, m * inv2


def terms(b, lo, up, v, rows, waves):
    apm, amp, flp, flm = rows[:4]
    w, dec, decz, cpl = waves
    sums = [lo[c] + up[c] for c in range(6)]
    swap = [None] * 6
    for k in range(3):
        swap[2 * k] = up[2 * k + 1] - lo[2 * k + 1]
        swap[2 * k + 1] = lo[2 * k] - up[2 * k]
    e = []
    for k in range(3):
        s, t = (k + 1) % 3, (k + 2) % 3
        for q in range(2):
            i, j = 2 * t + q, 2 * s + q
            e.append((v[s] * b[i] - v[t] * b[j]) + (v[3 + 2 * s] * sums[i] + v[4 + 2 * s] * swap[i])
                     - (v[3 + 2 * t] * sums[j] + v[4 + 2 * t] * swap[j]))
    local = [
        cpl * b[3] - w * e[5] - dec * b[0],
        w * e[4] - cpl * b[2] - dec * b[1],
        -(dec * b[2] + cpl * b[1]),
        cpl * b[0] - dec * b[3],
        w * e[1] - decz * b[4],
        -(w * e[0] + decz * b[5]),
    ]
    half_b = [0.5 * b[c] for c in range(6)]
    half_e = [0.5 * e[c] for c in range(6)]
    above, below, right, left = [], [], [], []
    for c in range(6):
        if c < 2:
            above.append(half_b[c] - half_e[2 + c])
            below.append(half_b[c] + half_e[2 + c])
        elif c < 4:
            above.append(half_b[c] + half_e[c - 2])
            below.append(half_b[c] - half_e[c - 2])
        else:
            above.append(half_b[c])
        right.append(apm * b[c])
        left.append(amp * b[c])
        if c in (2, 3):
            right[c] = right[c] - half_e[c + 2]
            left[c] = left[c] + half_e[c + 2]
        elif c >= 4:
            right[c] = right[c] + flp * e[c - 2]
            left[c] = left[c] - flm * e[c - 2]
    return local, above, below, right, left


def kernel(n_tile, wave_hbm, owner_hbm, mag, vel, out, S, T, Vin, M, R1, Q, R2, V, U, W, coef, P0, PL, PR, PV, VL, VR,
           VS, SX, ST, wave_ref, owner_ref, lsem, y_s, y_r, z_s, z_r, g_s, g_r, m_s, m_r, t_s, t_r, v_s, v_r, x_s, x_r):
    mode = lax.axis_index("mode")
    tile = lax.axis_index("tile")
    zc = mode // 4
    yc = mode % 4
    par = zc % 2
    zg = zc // 2

    load_w = pltpu.make_async_copy(wave_hbm, wave_ref, lsem.at[2])
    load_w.start()
    load_o = pltpu.make_async_copy(owner_hbm, owner_ref, lsem.at[3])
    load_o.start()
    load_v = pltpu.make_async_copy(vel.at[0], Vin, lsem.at[0])
    load_v.start()
    load_s = pltpu.make_async_copy(mag, S.at[pl.ds(4, 4)], lsem.at[1])
    load_s.start()

    mode_up = (mode + 1) % 32
    mode_dn = (mode + 31) % 32
    near = []
    for dp in range(2):
        for dy in range(4):
            if dp + dy:
                q, y = (par + dp) % 2, (yc + dy) % 4
                near.append((q, y, (2 * zg + q) * 4 + y))
    across = [(2 * ((zg + d) % 4) + par) * 4 + yc for d in (1, 2, 3)]
    has_up, has_dn = tile < n_tile - 1, tile > 0
    tile_up = (tile + 1) % n_tile
    tile_dn = (tile + n_tile - 1) % n_tile

    barrier = pltpu.get_barrier_semaphore()
    everyone = [(m, tile) for _, _, m in near] + [(m, tile) for m in across] + [(mode_up, tile), (mode_dn, tile), (mode, tile_up), (mode, tile_dn)]
    for where in everyone:
        pl.semaphore_signal(barrier, inc=1, device_id=where, device_id_type=MESH)
    lane = lax.broadcasted_iota(jnp.int32, (8, 128), 1)
    for i, row in enumerate(radius_rows(INNER + (tile * 128 + lane).astype(F32) + 0.5)):
        coef[0, i] = row
    place = lane % 32
    cell = jnp.where(place < 16, place - 8, place + 104) + tile * 128
    for i, row in enumerate(radius_rows(INNER + cell.astype(F32) + 0.5)):
        coef[1, i] = row
    zero = jnp.zeros((8, 128), F32)
    for c in range(6):
        for edge in (0, 40):
            U[c, edge:edge + 8, :] = zero
            if c < 4:
                W[c, edge:edge + 8, :] = zero

    @pl.when(tile == 0)
    def _():
        PL[...] = jnp.zeros_like(PL)
        VL[...] = jnp.zeros_like(VL)

    @pl.when(tile == n_tile - 1)
    def _():
        PR[...] = jnp.zeros_like(PR)
        VR[...] = jnp.zeros_like(VR)

    load_o.wait()
    load_w.wait()
    load_v.wait()
    mine = owner_ref[0] == mode
    M[0] = jnp.where(mine, Vin[0:5], 0.0)
    M[1] = jnp.where(mine, Vin[4:9], 0.0)
    pl.semaphore_wait(barrier, len(everyone))
    def remote(source, to, send, recv, where):
        return pltpu.make_async_remote_copy(source, to, send, recv, device_id=where, device_id_type=MESH)

    own = pl.ds(pl.multiple_of(yc * 8, 8), 8)
    spread, gather = [], []
    for i, (q, y, m) in enumerate(near):
        rows = pl.ds(pl.multiple_of(y * 8, 8), 8)
        spread.append(remote(M.at[q, :, rows, :], R1.at[i], y_s.at[i], y_r.at[i], (m, tile)))
        gather.append(remote(V.at[par, :, own, :], V.at[par, :, own, :], g_s.at[i], g_r.at[i], (m, tile)))
    for copy in spread:
        copy.start()

    halo = []
    for i in range(4):
        halo.append(remote(mag.at[3 - i], S.at[3 - i], m_s.at[2 * i], m_r.at[2 * i], (mode_up, tile)))
        halo.append(remote(mag.at[i], S.at[8 + i], m_s.at[2 * i + 1], m_r.at[2 * i + 1], (mode_dn, tile)))

    for copy in halo:
        copy.start()

    load_s.wait()
    eighth = place // 8

    @pl.loop(0, 6)
    def _(c):
        packed = zero
        for k in range(4):
            for zt in range(4):
                moved = pltpu.roll(S[4 + k, c, 8 * zt:8 * zt + 8, :], (4 + 32 * k + 8 * zt) % 128, 1)
                packed = jnp.where((eighth == zt) & (lane // 32 == k), moved, packed)
        P0[c] = packed

    to_up = remote(P0, PL, t_s.at[0], t_r.at[0], (mode, tile_up))
    to_dn = remote(P0, PR, t_s.at[1], t_r.at[1], (mode, tile_dn))
    v_up = remote(PV, VL, v_s.at[0], v_r.at[0], (mode, tile_up))
    v_dn = remote(PV, VR, v_s.at[1], v_r.at[1], (mode, tile_dn))

    @pl.when(has_up)
    def _():
        to_up.start()

    @pl.when(has_dn)
    def _():
        to_dn.start()

    total = M[par, :, own, :]
    for i in range(7):
        spread[i].wait_recv()
        total = total + R1[i]
    Q[...] = total
    middle = [remote(Q, R2.at[i], z_s.at[i], z_r.at[i], (across[i], tile)) for i in range(3)]
    for copy in middle:
        copy.start()

    total = Q[...]
    for i in range(3):
        middle[i].wait_recv()
        total = total + R2[i]
    V[par, :, own, :] = total
    for copy in gather:
        copy.start()
    for copy in gather:
        copy.wait_recv()

    def flow(f, zt):
        return V[f // 4 if f < 8 else 1, f % 4 if f < 8 else 4, 8 * zt:8 * zt + 8, :]

    for block in range(3):
        packed = zero
        for f in range(4 * block, min(9, 4 * block + 4)):
            for zt in range(4):
                i = 4 * (f % 4) + zt
                packed = jnp.where(lane // 8 == i, pltpu.roll(flow(f, zt), (4 + 8 * i) % 128, 1), packed)
        PV[block] = packed

    @pl.when(has_up)
    def _():
        v_up.start()

    @pl.when(has_dn)
    def _():
        v_dn.start()

    @pl.when(has_dn)
    def _():
        to_up.wait_recv()

    @pl.when(has_up)
    def _():
        to_dn.wait_recv()

    def strip(inner, outer, from_left, from_right):
        got = jnp.where((place >= 8) & (place < 16), inner, jnp.where((place >= 16) & (place < 24), outer, 0.0))
        got = jnp.where((place >= 4) & (place < 8), from_left, got)
        return jnp.where((place >= 24) & (place < 28), from_right, got)

    @pl.loop(0, 6)
    def _(c):
        for zt in range(4):
            rows = slice(8 * zt, 8 * zt + 8)
            inner, outer = zero, zero
            for k in range(4):
                s = S[4 + k, c, rows, :]
                inner = jnp.where(lane // 32 == k, pltpu.roll(s, (8 + 32 * k) % 128, 1), inner)
                outer = jnp.where(lane // 32 == k, pltpu.roll(s, (24 + 32 * k) % 128, 1), outer)
            SX[1, c, rows, :] = strip(inner, outer, pltpu.roll(PL[c], (4 - 8 * zt) % 128, 1),
                                      pltpu.roll(PR[c], (20 - 8 * zt) % 128, 1))

    strips = [remote(SX.at[1], SX.at[0], x_s.at[0], x_r.at[0], (mode_up, tile)),
              remote(SX.at[1], SX.at[2], x_s.at[1], x_r.at[1], (mode_dn, tile))]
    for copy in strips:
        copy.start()
    for copy in halo:
        copy.wait_recv()

    first_wave = wave_ref[0] + 64

    def evaluate(load, flows, rows, waves, base, target, step, blend, keep):
        for zt in range(4):
            span = slice(8 * zt, 8 * zt + 8)
            put = slice(8 + 8 * zt, 16 + 8 * zt)
            b, lo, up = load(span)
            local, above, below, right, left = terms(b, lo, up, flows(zt), rows, waves)
            for c in range(6):
                U[c, put, :] = above[c]
                if c < 4:
                    W[c, put, :] = below[c]
                partial = local[c] + pltpu.roll(right[c], 127, 1) + pltpu.roll(left[c], 1, 1)
                start = base[c, span, :]
                if blend:
                    start = 0.5 * start + 0.5 * b[c]
                target[c, span, :] = start + step * partial
        for c in range(6):
            low = U if c >= 4 else W
            for zt in range(4):
                span = slice(8 * zt, 8 * zt + 8)
                moved = U[c, 9 + 8 * zt:17 + 8 * zt, :] + low[c, 7 + 8 * zt:15 + 8 * zt, :]
                target[c, span, :] = keep(target[c, span, :] + step * moved)

    for e in range(4):
        cur, target = (S, T) if e % 2 == 0 else (T, S)
        shift = 0
        if e == 3:
            target, shift = out, 4
        step = TIME_STEP if e % 2 == 0 else 0.5 * TIME_STEP

        @pl.loop(e + 1, 11 - e)
        def _(slot, cur=cur, target=target, shift=shift, step=step, e=e):
            m = (((first_wave + (slot - 4) + 128) & 127) - 64).astype(F32)
            rows = [coef[0, i] for i in range(6)]

            def load(span):
                return [[cur[s, c, span, :] for c in range(6)] for s in (slot, slot - 1, slot + 1)]

            evaluate(load, lambda zt: [flow(f, zt) for f in range(9)], rows, wave_rows(m, rows),
                     S.at[slot], target.at[slot - shift], step, e % 2 == 1, lambda x: x)

    @pl.when(has_dn)
    def _():
        v_up.wait_recv()

    @pl.when(has_up)
    def _():
        v_dn.wait_recv()

    for f in range(9):
        for zt in range(4):
            i = 4 * (f % 4) + zt
            mine = flow(f, zt)
            x = strip(pltpu.roll(mine, 8, 1), pltpu.roll(mine, 24, 1), pltpu.roll(VL[f // 4], (4 - 8 * i) % 128, 1),
                      pltpu.roll(VR[f // 4], (20 - 8 * i) % 128, 1))
            x = jnp.where(lane < 32, x, pltpu.roll(x, 32, 1))
            VS[f, 8 * zt:8 * zt + 8, :] = jnp.where(lane < 64, x, pltpu.roll(x, 64, 1))

    for copy in strips:
        copy.wait_recv()
        copy.wait_send()

    inside = (cell >= 0) & (cell < n_tile * 128)
    for e in range(4):
        cur, target = (SX, ST) if e % 2 == 0 else (ST, SX)
        step = TIME_STEP if e % 2 == 0 else 0.5 * TIME_STEP

        @pl.loop(0 if e < 3 else 1, 3 if e < 3 else 2)
        def _(g, cur=cur, target=target, step=step, e=e):
            m = (((first_wave + (4 * g - 4 + lane // 32) + 128) & 127) - 64).astype(F32)
            rows = [coef[1, i] for i in range(6)]

            def load(span):
                b = [cur[g, c, span, :] for c in range(6)]
                lo = [pltpu.roll(jnp.where(lane >= 96, cur[(g + 2) % 3, c, span, :], b[c]), 32, 1) for c in range(6)]
                up = [pltpu.roll(jnp.where(lane < 32, cur[(g + 1) % 3, c, span, :], b[c]), 96, 1) for c in range(6)]
                return b, lo, up

            evaluate(load, lambda zt: [VS[f, 8 * zt:8 * zt + 8, :] for f in range(9)], rows, wave_rows(m, rows),
                     SX.at[g], target.at[g], step, e % 2 == 1, lambda x: jnp.where(inside, x, 0.0))

    @pl.loop(0, 6)
    def _(c):
        for zt in range(4):
            rows = slice(8 * zt, 8 * zt + 8)
            s = SX[1, c, rows, :]
            for k in range(4):
                edge = jnp.where(lane < 4, pltpu.roll(s, (120 - 32 * k) % 128, 1), out[k, c, rows, :])
                out[k, c, rows, :] = jnp.where(lane >= 124, pltpu.roll(s, (104 - 32 * k) % 128, 1), edge)

    for copy in spread + middle + gather + halo:
        copy.wait_send()

    @pl.when(has_up)
    def _():
        to_up.wait_send()
        v_up.wait_send()

    @pl.when(has_dn)
    def _():
        to_dn.wait_send()
        v_dn.wait_send()


def body(n_tile, magnetic, velocity_stack, wavenumber, velocity_owner):
    vmem = pl.BlockSpec(memory_space=pltpu.VMEM)
    hbm = pl.BlockSpec(memory_space=pltpu.HBM)

    def dma(n):
        return pltpu.SemaphoreType.DMA((n,))

    def room(*shape):
        return pltpu.VMEM(shape, F32)

    return pl.pallas_call(
        functools.partial(kernel, n_tile),
        out_shape=jax.ShapeDtypeStruct((4, 6, 32, 128), F32),
        in_specs=[hbm, hbm, hbm, hbm],
        out_specs=vmem,
        scratch_shapes=[
            room(12, 6, 32, 128), room(12, 6, 32, 128), room(9, 32, 128), room(2, 5, 32, 128),
            room(7, 5, 8, 128), room(5, 8, 128), room(3, 5, 8, 128), room(2, 5, 32, 128),
            room(6, 48, 128), room(4, 48, 128), room(2, 6, 8, 128),
            room(6, 8, 128), room(6, 8, 128), room(6, 8, 128), room(3, 8, 128), room(3, 8, 128), room(3, 8, 128),
            room(9, 32, 128), room(3, 6, 32, 128), room(3, 6, 32, 128),
            pltpu.SMEM((4,), jnp.int32), pltpu.SMEM((1,), jnp.int32),
            dma(4), dma(7), dma(7), dma(3), dma(3), dma(7), dma(7), dma(8), dma(8),
            dma(2), dma(2), dma(2), dma(2), dma(2), dma(2),
        ],
        compiler_params=pltpu.CompilerParams(collective_id=0, has_side_effects=True, vmem_limit_bytes=32 << 20),
    )(wavenumber, velocity_owner, magnetic, velocity_stack)


def solution(mesh):
    placed = (P("mode", None, None, "tile"), P("mode", None, None, "tile"), P("mode"), P())
    return jax.shard_map(
        functools.partial(body, mesh.shape["tile"]), mesh=mesh, in_specs=placed,
        out_specs=P("mode", None, None, "tile"), check_vma=False,
    )
```

```python
import functools

import jax
import jax.numpy as jnp
from jax import lax
from jax.experimental import pallas as pl
from jax.experimental.pallas import tpu as pltpu
from jax.sharding import PartitionSpec as P

MESH = pl.DeviceIdType.MESH
TIME_STEP = 0.2
INNER = 32.0
F32 = jnp.float32


def radius_rows(radius):
    before, after = radius - 1.0, radius + 1.0
    return [0.5 + 0.25 / before, 0.5 - 0.25 / after, 0.5 * radius / before, 0.5 * radius / after,
            1.0 / radius, 1.0 / (radius * radius)]


def wave_rows(m, rows):
    inv, inv2 = rows[4], rows[5]
    return m * inv, 2.0 + (0.5 * (m * m + 1.0)) * inv2, 2.0 + (0.5 * (m * m)) * inv2, m * inv2


def terms(b, lo, up, v, rows, waves):
    apm, amp, flp, flm = rows[:4]
    w, dec, decz, cpl = waves
    sums = [lo[c] + up[c] for c in range(6)]
    swap = [None] * 6
    for k in range(3):
        swap[2 * k] = up[2 * k + 1] - lo[2 * k + 1]
        swap[2 * k + 1] = lo[2 * k] - up[2 * k]
    e = []
    for k in range(3):
        s, t = (k + 1) % 3, (k + 2) % 3
        for q in range(2):
            i, j = 2 * t + q, 2 * s + q
            e.append((v[s] * b[i] - v[t] * b[j]) + (v[3 + 2 * s] * sums[i] + v[4 + 2 * s] * swap[i])
                     - (v[3 + 2 * t] * sums[j] + v[4 + 2 * t] * swap[j]))
    local = [
        cpl * b[3] - w * e[5] - dec * b[0],
        w * e[4] - cpl * b[2] - dec * b[1],
        -(dec * b[2] + cpl * b[1]),
        cpl * b[0] - dec * b[3],
        w * e[1] - decz * b[4],
        -(w * e[0] + decz * b[5]),
    ]
    half_b = [0.5 * b[c] for c in range(6)]
    half_e = [0.5 * e[c] for c in range(6)]
    above, below, right, left = [], [], [], []
    for c in range(6):
        if c < 2:
            above.append(half_b[c] - half_e[2 + c])
            below.append(half_b[c] + half_e[2 + c])
        elif c < 4:
            above.append(half_b[c] + half_e[c - 2])
            below.append(half_b[c] - half_e[c - 2])
        else:
            above.append(half_b[c])
        right.append(apm * b[c])
        left.append(amp * b[c])
        if c in (2, 3):
            right[c] = right[c] - half_e[c + 2]
            left[c] = left[c] + half_e[c + 2]
        elif c >= 4:
            right[c] = right[c] + flp * e[c - 2]
            left[c] = left[c] - flm * e[c - 2]
    return local, above, below, right, left


def kernel(n_tile, wave_hbm, owner_hbm, mag, vel, out, S, T, Vin, M, R1, Q, R2, V, U, W, coef, P0, PL, PR, PV, VL, VR,
           VS, SX, ST, RB, r_s, r_r, f_s, wave_ref, owner_ref, lsem, y_s, y_r, z_s, z_r, g_s, g_r, m_s, m_r, t_s, t_r, v_s, v_r, x_s, x_r):
    mode = lax.axis_index("mode")
    tile = lax.axis_index("tile")
    zc = mode // 4
    yc = mode % 4
    par = zc % 2
    zg = zc // 2

    load_w = pltpu.make_async_copy(wave_hbm, wave_ref, lsem.at[2])
    load_w.start()
    load_o = pltpu.make_async_copy(owner_hbm, owner_ref, lsem.at[3])
    load_o.start()
    load_v = pltpu.make_async_copy(vel.at[0], Vin, lsem.at[0])
    load_v.start()
    load_s = pltpu.make_async_copy(mag, S.at[pl.ds(4, 4)], lsem.at[1])
    load_s.start()

    mode_up = (mode + 1) % 32
    mode_dn = (mode + 31) % 32
    mode_next = (mode + 4) % 32
    mode_prev = (mode + 28) % 32
    near = []
    for dp in range(2):
        for dy in range(4):
            if dp + dy:
                q, y = (par + dp) % 2, (yc + dy) % 4
                near.append((q, y, (2 * zg + q) * 4 + y))
    across = [(2 * ((zg + d) % 4) + par) * 4 + yc for d in (1, 2, 3)]
    has_up, has_dn = tile < n_tile - 1, tile > 0
    tile_up = (tile + 1) % n_tile
    tile_dn = (tile + n_tile - 1) % n_tile

    barrier = pltpu.get_barrier_semaphore()
    everyone = [(m, tile) for _, _, m in near] + [(m, tile) for m in across] + [(mode_up, tile), (mode_dn, tile), (mode, tile_up), (mode, tile_dn)]
    everyone += [(mode_next, tile), (mode_prev, tile)]
    for where in everyone:
        pl.semaphore_signal(barrier, inc=1, device_id=where, device_id_type=MESH)
    lane = lax.broadcasted_iota(jnp.int32, (8, 128), 1)
    for i, row in enumerate(radius_rows(INNER + (tile * 128 + lane).astype(F32) + 0.5)):
        coef[0, i] = row
    place = lane % 32
    cell = jnp.where(place < 16, place - 8, place + 104) + tile * 128
    for i, row in enumerate(radius_rows(INNER + cell.astype(F32) + 0.5)):
        coef[1, i] = row
    zero = jnp.zeros((8, 128), F32)
    for c in range(6):
        for edge in (0, 40):
            U[c, edge:edge + 8, :] = zero
            if c < 4:
                W[c, edge:edge + 8, :] = zero

    @pl.when(tile == 0)
    def _():
        PL[...] = jnp.zeros_like(PL)
        VL[...] = jnp.zeros_like(VL)

    @pl.when(tile == n_tile - 1)
    def _():
        PR[...] = jnp.zeros_like(PR)
        VR[...] = jnp.zeros_like(VR)

    load_o.wait()
    load_w.wait()
    load_v.wait()
    mine = owner_ref[0] == mode
    M[0] = jnp.where(mine, Vin[0:5], 0.0)
    M[1] = jnp.where(mine, Vin[4:9], 0.0)
    pl.semaphore_wait(barrier, len(everyone))
    def remote(source, to, send, recv, where):
        return pltpu.make_async_remote_copy(source, to, send, recv, device_id=where, device_id_type=MESH)

    own = pl.ds(pl.multiple_of(yc * 8, 8), 8)
    spread, gather = [], []
    for i, (q, y, m) in enumerate(near):
        rows = pl.ds(pl.multiple_of(y * 8, 8), 8)
        spread.append(remote(M.at[q, :, rows, :], R1.at[i], y_s.at[i], y_r.at[i], (m, tile)))
        gather.append(remote(V.at[par, :, own, :], V.at[par, :, own, :], g_s.at[i], g_r.at[i], (m, tile)))
    for copy in spread:
        copy.start()

    halo = []
    for i in range(4):
        halo.append(remote(mag.at[3 - i], S.at[3 - i], m_s.at[2 * i], m_r.at[2 * i], (mode_up, tile)))
        halo.append(remote(mag.at[i], S.at[8 + i], m_s.at[2 * i + 1], m_r.at[2 * i + 1], (mode_dn, tile)))

    for copy in halo[:4]:
        copy.start()
    by_up, by_dn, on_top, on_low = [], [], [], []
    for j in range(2):
        i = 2 + j
        by_up.append(remote(mag.at[3 - i], RB.at[j], r_s.at[j], r_r.at[j], ((mode + 29) % 32, tile)))
        by_dn.append(remote(mag.at[i], RB.at[j], r_s.at[j], r_r.at[j], ((mode + 3) % 32, tile)))
        on_top.append(remote(RB.at[j], S.at[8 + i], f_s.at[j], m_r.at[2 * i + 1], (mode_prev, tile)))
        on_low.append(remote(RB.at[j], S.at[3 - i], f_s.at[j], m_r.at[2 * i], (mode_next, tile)))
    top, low = yc == 3, yc == 0

    @pl.when(top)
    def _():
        for copy in by_up:
            copy.start()

    @pl.when(yc != 3)
    def _():
        for copy in halo[4::2]:
            copy.start()

    @pl.when(low)
    def _():
        for copy in by_dn:
            copy.start()

    @pl.when(yc != 0)
    def _():
        for copy in halo[5::2]:
            copy.start()


    load_s.wait()
    eighth = place // 8

    @pl.loop(0, 6)
    def _(c):
        packed = zero
        for k in range(4):
            for zt in range(4):
                moved = pltpu.roll(S[4 + k, c, 8 * zt:8 * zt + 8, :], (4 + 32 * k + 8 * zt) % 128, 1)
                packed = jnp.where((eighth == zt) & (lane // 32 == k), moved, packed)
        P0[c] = packed

    to_up = remote(P0, PL, t_s.at[0], t_r.at[0], (mode, tile_up))
    to_dn = remote(P0, PR, t_s.at[1], t_r.at[1], (mode, tile_dn))
    v_up = remote(PV, VL, v_s.at[0], v_r.at[0], (mode, tile_up))
    v_dn = remote(PV, VR, v_s.at[1], v_r.at[1], (mode, tile_dn))

    @pl.when(has_up)
    def _():
        to_up.start()

    @pl.when(has_dn)
    def _():
        to_dn.start()

    total = M[par, :, own, :]
    for i in range(7):
        spread[i].wait_recv()
        total = total + R1[i]
    Q[...] = total
    middle = [remote(Q, R2.at[i], z_s.at[i], z_r.at[i], (across[i], tile)) for i in range(3)]
    for copy in middle:
        copy.start()

    @pl.when(top)
    def _():
        for j in range(2):
            by_up[j].wait_recv()
            on_top[j].start()

    @pl.when(low)
    def _():
        for j in range(2):
            by_dn[j].wait_recv()
            on_low[j].start()


    total = Q[...]
    for i in range(3):
        middle[i].wait_recv()
        total = total + R2[i]
    V[par, :, own, :] = total
    for copy in gather:
        copy.start()
    for copy in gather:
        copy.wait_recv()

    def flow(f, zt):
        return V[f // 4 if f < 8 else 1, f % 4 if f < 8 else 4, 8 * zt:8 * zt + 8, :]

    for block in range(3):
        packed = zero
        for f in range(4 * block, min(9, 4 * block + 4)):
            for zt in range(4):
                i = 4 * (f % 4) + zt
                packed = jnp.where(lane // 8 == i, pltpu.roll(flow(f, zt), (4 + 8 * i) % 128, 1), packed)
        PV[block] = packed

    @pl.when(has_up)
    def _():
        v_up.start()

    @pl.when(has_dn)
    def _():
        v_dn.start()

    @pl.when(has_dn)
    def _():
        to_up.wait_recv()

    @pl.when(has_up)
    def _():
        to_dn.wait_recv()

    def strip(inner, outer, from_left, from_right):
        got = jnp.where((place >= 8) & (place < 16), inner, jnp.where((place >= 16) & (place < 24), outer, 0.0))
        got = jnp.where((place >= 4) & (place < 8), from_left, got)
        return jnp.where((place >= 24) & (place < 28), from_right, got)

    @pl.loop(0, 6)
    def _(c):
        for zt in range(4):
            rows = slice(8 * zt, 8 * zt + 8)
            inner, outer = zero, zero
            for k in range(4):
                s = S[4 + k, c, rows, :]
                inner = jnp.where(lane // 32 == k, pltpu.roll(s, (8 + 32 * k) % 128, 1), inner)
                outer = jnp.where(lane // 32 == k, pltpu.roll(s, (24 + 32 * k) % 128, 1), outer)
            SX[1, c, rows, :] = strip(inner, outer, pltpu.roll(PL[c], (4 - 8 * zt) % 128, 1),
                                      pltpu.roll(PR[c], (20 - 8 * zt) % 128, 1))

    strips = [remote(SX.at[1], SX.at[0], x_s.at[0], x_r.at[0], (mode_up, tile)),
              remote(SX.at[1], SX.at[2], x_s.at[1], x_r.at[1], (mode_dn, tile))]
    for copy in strips:
        copy.start()
    for copy in halo:
        copy.wait_recv()

    first_wave = wave_ref[0] + 64

    def evaluate(load, flows, rows, waves, base, target, step, blend, keep):
        for zt in range(4):
            span = slice(8 * zt, 8 * zt + 8)
            put = slice(8 + 8 * zt, 16 + 8 * zt)
            b, lo, up = load(span)
            local, above, below, right, left = terms(b, lo, up, flows(zt), rows, waves)
            for c in range(6):
                U[c, put, :] = above[c]
                if c < 4:
                    W[c, put, :] = below[c]
                partial = local[c] + pltpu.roll(right[c], 127, 1) + pltpu.roll(left[c], 1, 1)
                start = base[c, span, :]
                if blend:
                    start = 0.5 * start + 0.5 * b[c]
                target[c, span, :] = start + step * partial
        for c in range(6):
            low = U if c >= 4 else W
            for zt in range(4):
                span = slice(8 * zt, 8 * zt + 8)
                moved = U[c, 9 + 8 * zt:17 + 8 * zt, :] + low[c, 7 + 8 * zt:15 + 8 * zt, :]
                target[c, span, :] = keep(target[c, span, :] + step * moved)

    for e in range(4):
        cur, target = (S, T) if e % 2 == 0 else (T, S)
        shift = 0
        if e == 3:
            target, shift = out, 4
        step = TIME_STEP if e % 2 == 0 else 0.5 * TIME_STEP

        @pl.loop(e + 1, 11 - e)
        def _(slot, cur=cur, target=target, shift=shift, step=step, e=e):
            m = (((first_wave + (slot - 4) + 128) & 127) - 64).astype(F32)
            rows = [coef[0, i] for i in range(6)]

            def load(span):
                return [[cur[s, c, span, :] for c in range(6)] for s in (slot, slot - 1, slot + 1)]

            evaluate(load, lambda zt: [flow(f, zt) for f in range(9)], rows, wave_rows(m, rows),
                     S.at[slot], target.at[slot - shift], step, e % 2 == 1, lambda x: x)

    @pl.when(has_dn)
    def _():
        v_up.wait_recv()

    @pl.when(has_up)
    def _():
        v_dn.wait_recv()

    for f in range(9):
        for zt in range(4):
            i = 4 * (f % 4) + zt
            mine = flow(f, zt)
            x = strip(pltpu.roll(mine, 8, 1), pltpu.roll(mine, 24, 1), pltpu.roll(VL[f // 4], (4 - 8 * i) % 128, 1),
                      pltpu.roll(VR[f // 4], (20 - 8 * i) % 128, 1))
            x = jnp.where(lane < 32, x, pltpu.roll(x, 32, 1))
            VS[f, 8 * zt:8 * zt + 8, :] = jnp.where(lane < 64, x, pltpu.roll(x, 64, 1))

    for copy in strips:
        copy.wait_recv()
        copy.wait_send()

    inside = (cell >= 0) & (cell < n_tile * 128)
    for e in range(4):
        cur, target = (SX, ST) if e % 2 == 0 else (ST, SX)
        step = TIME_STEP if e % 2 == 0 else 0.5 * TIME_STEP

        @pl.loop(0 if e < 3 else 1, 3 if e < 3 else 2)
        def _(g, cur=cur, target=target, step=step, e=e):
            m = (((first_wave + (4 * g - 4 + lane // 32) + 128) & 127) - 64).astype(F32)
            rows = [coef[1, i] for i in range(6)]

            def load(span):
                b = [cur[g, c, span, :] for c in range(6)]
                lo = [pltpu.roll(jnp.where(lane >= 96, cur[(g + 2) % 3, c, span, :], b[c]), 32, 1) for c in range(6)]
                up = [pltpu.roll(jnp.where(lane < 32, cur[(g + 1) % 3, c, span, :], b[c]), 96, 1) for c in range(6)]
                return b, lo, up

            evaluate(load, lambda zt: [VS[f, 8 * zt:8 * zt + 8, :] for f in range(9)], rows, wave_rows(m, rows),
                     SX.at[g], target.at[g], step, e % 2 == 1, lambda x: jnp.where(inside, x, 0.0))

    @pl.loop(0, 6)
    def _(c):
        for zt in range(4):
            rows = slice(8 * zt, 8 * zt + 8)
            s = SX[1, c, rows, :]
            for k in range(4):
                edge = jnp.where(lane < 4, pltpu.roll(s, (120 - 32 * k) % 128, 1), out[k, c, rows, :])
                out[k, c, rows, :] = jnp.where(lane >= 124, pltpu.roll(s, (104 - 32 * k) % 128, 1), edge)

    for copy in spread + middle + gather + halo[:4]:
        copy.wait_send()

    @pl.when(top)
    def _():
        for copy in by_up + on_top:
            copy.wait_send()

    @pl.when(yc != 3)
    def _():
        for copy in halo[4::2]:
            copy.wait_send()

    @pl.when(low)
    def _():
        for copy in by_dn + on_low:
            copy.wait_send()

    @pl.when(yc != 0)
    def _():
        for copy in halo[5::2]:
            copy.wait_send()

    @pl.when(has_up)
    def _():
        to_up.wait_send()
        v_up.wait_send()

    @pl.when(has_dn)
    def _():
        to_dn.wait_send()
        v_dn.wait_send()


def body(n_tile, magnetic, velocity_stack, wavenumber, velocity_owner):
    vmem = pl.BlockSpec(memory_space=pltpu.VMEM)
    hbm = pl.BlockSpec(memory_space=pltpu.HBM)

    def dma(n):
        return pltpu.SemaphoreType.DMA((n,))

    def room(*shape):
        return pltpu.VMEM(shape, F32)

    return pl.pallas_call(
        functools.partial(kernel, n_tile),
        out_shape=jax.ShapeDtypeStruct((4, 6, 32, 128), F32),
        in_specs=[hbm, hbm, hbm, hbm],
        out_specs=vmem,
        scratch_shapes=[
            room(12, 6, 32, 128), room(12, 6, 32, 128), room(9, 32, 128), room(2, 5, 32, 128),
            room(7, 5, 8, 128), room(5, 8, 128), room(3, 5, 8, 128), room(2, 5, 32, 128),
            room(6, 48, 128), room(4, 48, 128), room(2, 6, 8, 128),
            room(6, 8, 128), room(6, 8, 128), room(6, 8, 128), room(3, 8, 128), room(3, 8, 128), room(3, 8, 128),
            room(9, 32, 128), room(3, 6, 32, 128), room(3, 6, 32, 128), room(2, 6, 32, 128), dma(2), dma(2), dma(2),
            pltpu.SMEM((4,), jnp.int32), pltpu.SMEM((1,), jnp.int32),
            dma(4), dma(7), dma(7), dma(3), dma(3), dma(7), dma(7), dma(8), dma(8),
            dma(2), dma(2), dma(2), dma(2), dma(2), dma(2),
        ],
        compiler_params=pltpu.CompilerParams(collective_id=0, has_side_effects=True, vmem_limit_bytes=60 << 20),
    )(wavenumber, velocity_owner, magnetic, velocity_stack)


def solution(mesh):
    placed = (P("mode", None, None, "tile"), P("mode", None, None, "tile"), P("mode"), P())
    return jax.shard_map(
        functools.partial(body, mesh.shape["tile"]), mesh=mesh, in_specs=placed,
        out_specs=P("mode", None, None, "tile"), check_vma=False,
    )
```

```python
import functools

import jax
import jax.numpy as jnp
from jax import lax
from jax.experimental import pallas as pl
from jax.experimental.pallas import tpu as pltpu
from jax.sharding import PartitionSpec as P

MESH = pl.DeviceIdType.MESH
TIME_STEP = 0.2
INNER = 32.0
F32 = jnp.float32


def radius_rows(radius):
    before, after = radius - 1.0, radius + 1.0
    return [0.5 + 0.25 / before, 0.5 - 0.25 / after, 0.5 * radius / before, 0.5 * radius / after,
            1.0 / radius, 1.0 / (radius * radius)]


def wave_rows(m, rows):
    inv, inv2 = rows[4], rows[5]
    return m * inv, 2.0 + (0.5 * (m * m + 1.0)) * inv2, 2.0 + (0.5 * (m * m)) * inv2, m * inv2


def terms(b, lo, up, v, rows, waves):
    apm, amp, flp, flm = rows[:4]
    w, dec, decz, cpl = waves
    sums = [lo[c] + up[c] for c in range(6)]
    swap = [None] * 6
    for k in range(3):
        swap[2 * k] = up[2 * k + 1] - lo[2 * k + 1]
        swap[2 * k + 1] = lo[2 * k] - up[2 * k]
    e = []
    for k in range(3):
        s, t = (k + 1) % 3, (k + 2) % 3
        for q in range(2):
            i, j = 2 * t + q, 2 * s + q
            e.append((v[s] * b[i] - v[t] * b[j]) + (v[3 + 2 * s] * sums[i] + v[4 + 2 * s] * swap[i])
                     - (v[3 + 2 * t] * sums[j] + v[4 + 2 * t] * swap[j]))
    local = [
        cpl * b[3] - w * e[5] - dec * b[0],
        w * e[4] - cpl * b[2] - dec * b[1],
        -(dec * b[2] + cpl * b[1]),
        cpl * b[0] - dec * b[3],
        w * e[1] - decz * b[4],
        -(w * e[0] + decz * b[5]),
    ]
    half_b = [0.5 * b[c] for c in range(6)]
    half_e = [0.5 * e[c] for c in range(6)]
    above, below, right, left = [], [], [], []
    for c in range(6):
        if c < 2:
            above.append(half_b[c] - half_e[2 + c])
            below.append(half_b[c] + half_e[2 + c])
        elif c < 4:
            above.append(half_b[c] + half_e[c - 2])
            below.append(half_b[c] - half_e[c - 2])
        else:
            above.append(half_b[c])
        right.append(apm * b[c])
        left.append(amp * b[c])
        if c in (2, 3):
            right[c] = right[c] - half_e[c + 2]
            left[c] = left[c] + half_e[c + 2]
        elif c >= 4:
            right[c] = right[c] + flp * e[c - 2]
            left[c] = left[c] - flm * e[c - 2]
    return local, above, below, right, left


def kernel(n_tile, wave_hbm, owner_hbm, mag, vel, out, S, T, Vin, M, R1, Q, R2, V, U, W, coef, P0, PL, PR, PV, VL, VR,
           VS, SX, ST, RB, r_s, r_r, f_s, wave_ref, owner_ref, lsem, y_s, y_r, z_s, z_r, g_s, g_r, m_s, m_r, t_s, t_r, v_s, v_r, x_s, x_r):
    mode = lax.axis_index("mode")
    tile = lax.axis_index("tile")
    zc = mode // 4
    yc = mode % 4
    par = zc % 2
    zg = zc // 2

    load_w = pltpu.make_async_copy(wave_hbm, wave_ref, lsem.at[2])
    load_w.start()
    load_o = pltpu.make_async_copy(owner_hbm, owner_ref, lsem.at[3])
    load_o.start()
    load_v = pltpu.make_async_copy(vel.at[0], Vin, lsem.at[0])
    load_v.start()
    load_s = pltpu.make_async_copy(mag, S.at[pl.ds(4, 4)], lsem.at[1])
    load_s.start()

    mode_up = (mode + 1) % 32
    mode_dn = (mode + 31) % 32
    mode_next = (mode + 4) % 32
    mode_prev = (mode + 28) % 32
    near = []
    for dp in range(2):
        for dy in range(4):
            if dp + dy:
                q, y = (par + dp) % 2, (yc + dy) % 4
                near.append((q, y, (2 * zg + q) * 4 + y))
    across = [(2 * ((zg + d) % 4) + par) * 4 + yc for d in (1, 2, 3)]
    has_up, has_dn = tile < n_tile - 1, tile > 0
    tile_up = (tile + 1) % n_tile
    tile_dn = (tile + n_tile - 1) % n_tile

    barrier = pltpu.get_barrier_semaphore()
    everyone = [(m, tile) for _, _, m in near] + [(m, tile) for m in across] + [(mode_up, tile), (mode_dn, tile), (mode, tile_up), (mode, tile_dn)]
    everyone += [(mode_next, tile), (mode_prev, tile)]
    for where in everyone:
        pl.semaphore_signal(barrier, inc=1, device_id=where, device_id_type=MESH)
    lane = lax.broadcasted_iota(jnp.int32, (8, 128), 1)
    for i, row in enumerate(radius_rows(INNER + (tile * 128 + lane).astype(F32) + 0.5)):
        coef[0, i] = row
    place = lane % 32
    cell = jnp.where(place < 16, place - 8, place + 104) + tile * 128
    for i, row in enumerate(radius_rows(INNER + cell.astype(F32) + 0.5)):
        coef[1, i] = row
    zero = jnp.zeros((8, 128), F32)
    for c in range(6):
        for edge in (0, 40):
            U[c, edge:edge + 8, :] = zero
            if c < 4:
                W[c, edge:edge + 8, :] = zero

    @pl.when(tile == 0)
    def _():
        PL[...] = jnp.zeros_like(PL)
        VL[...] = jnp.zeros_like(VL)

    @pl.when(tile == n_tile - 1)
    def _():
        PR[...] = jnp.zeros_like(PR)
        VR[...] = jnp.zeros_like(VR)

    load_o.wait()
    load_w.wait()
    load_v.wait()
    mine = owner_ref[0] == mode
    M[0] = jnp.where(mine, Vin[0:5], 0.0)
    M[1] = jnp.where(mine, Vin[4:9], 0.0)
    pl.semaphore_wait(barrier, len(everyone))
    def remote(source, to, send, recv, where):
        return pltpu.make_async_remote_copy(source, to, send, recv, device_id=where, device_id_type=MESH)

    own = pl.ds(pl.multiple_of(yc * 8, 8), 8)
    spread, gather = [], []
    for i, (q, y, m) in enumerate(near):
        rows = pl.ds(pl.multiple_of(y * 8, 8), 8)
        spread.append(remote(M.at[q, :, rows, :], R1.at[i], y_s.at[i], y_r.at[i], (m, tile)))
        gather.append(remote(V.at[par, :, own, :], V.at[par, :, own, :], g_s.at[i], g_r.at[i], (m, tile)))
    for copy in spread:
        copy.start()

    halo = []
    for i in range(4):
        halo.append(remote(mag.at[3 - i], S.at[3 - i], m_s.at[2 * i], m_r.at[2 * i], (mode_up, tile)))
        halo.append(remote(mag.at[i], S.at[8 + i], m_s.at[2 * i + 1], m_r.at[2 * i + 1], (mode_dn, tile)))

    for copy in halo[:4]:
        copy.start()
    by_up, by_dn, on_top, on_low = [], [], [], []
    for j in range(2):
        i = 2 + j
        by_up.append(remote(mag.at[3 - i], RB.at[j], r_s.at[j], r_r.at[j], ((mode + 29) % 32, tile)))
        by_dn.append(remote(mag.at[i], RB.at[j], r_s.at[j], r_r.at[j], ((mode + 3) % 32, tile)))
        on_top.append(remote(RB.at[j], S.at[8 + i], f_s.at[j], m_r.at[2 * i + 1], (mode_prev, tile)))
        on_low.append(remote(RB.at[j], S.at[3 - i], f_s.at[j], m_r.at[2 * i], (mode_next, tile)))
    top, low = yc == 3, yc == 0

    @pl.when(top)
    def _():
        for copy in by_up:
            copy.start()

    @pl.when(yc != 3)
    def _():
        for copy in halo[4::2]:
            copy.start()

    @pl.when(low)
    def _():
        for copy in by_dn:
            copy.start()

    @pl.when(yc != 0)
    def _():
        for copy in halo[5::2]:
            copy.start()


    load_s.wait()
    eighth = place // 8

    @pl.loop(0, 6)
    def _(c):
        packed = zero
        for k in range(4):
            for zt in range(4):
                moved = pltpu.roll(S[4 + k, c, 8 * zt:8 * zt + 8, :], (4 + 32 * k + 8 * zt) % 128, 1)
                packed = jnp.where((eighth == zt) & (lane // 32 == k), moved, packed)
        P0[c] = packed

    to_up = remote(P0, PL, t_s.at[0], t_r.at[0], (mode, tile_up))
    to_dn = remote(P0, PR, t_s.at[1], t_r.at[1], (mode, tile_dn))
    v_up = remote(PV, VL, v_s.at[0], v_r.at[0], (mode, tile_up))
    v_dn = remote(PV, VR, v_s.at[1], v_r.at[1], (mode, tile_dn))

    @pl.when(has_up)
    def _():
        to_up.start()

    @pl.when(has_dn)
    def _():
        to_dn.start()

    total = M[par, :, own, :]
    for i in range(7):
        spread[i].wait_recv()
        total = total + R1[i]
    Q[...] = total
    middle = [remote(Q, R2.at[i], z_s.at[i], z_r.at[i], (across[i], tile)) for i in range(3)]
    for copy in middle:
        copy.start()

    @pl.when(top)
    def _():
        for j in range(2):
            by_up[j].wait_recv()
            on_top[j].start()

    @pl.when(low)
    def _():
        for j in range(2):
            by_dn[j].wait_recv()
            on_low[j].start()


    total = Q[...]
    for i in range(3):
        middle[i].wait_recv()
        total = total + R2[i]
    V[par, :, own, :] = total
    for copy in gather:
        copy.start()
    for copy in gather:
        copy.wait_recv()

    def flow(f, zt):
        return V[f // 4 if f < 8 else 1, f % 4 if f < 8 else 4, 8 * zt:8 * zt + 8, :]

    for block in range(3):
        packed = zero
        for f in range(4 * block, min(9, 4 * block + 4)):
            for zt in range(4):
                i = 4 * (f % 4) + zt
                packed = jnp.where(lane // 8 == i, pltpu.roll(flow(f, zt), (4 + 8 * i) % 128, 1), packed)
        PV[block] = packed

    @pl.when(has_up)
    def _():
        v_up.start()

    @pl.when(has_dn)
    def _():
        v_dn.start()

    @pl.when(has_dn)
    def _():
        to_up.wait_recv()

    @pl.when(has_up)
    def _():
        to_dn.wait_recv()

    def strip(inner, outer, from_left, from_right):
        got = jnp.where((place >= 8) & (place < 16), inner, jnp.where((place >= 16) & (place < 24), outer, 0.0))
        got = jnp.where((place >= 4) & (place < 8), from_left, got)
        return jnp.where((place >= 24) & (place < 28), from_right, got)

    @pl.loop(0, 6)
    def _(c):
        for zt in range(4):
            rows = slice(8 * zt, 8 * zt + 8)
            inner, outer = zero, zero
            for k in range(4):
                s = S[4 + k, c, rows, :]
                inner = jnp.where(lane // 32 == k, pltpu.roll(s, (8 + 32 * k) % 128, 1), inner)
                outer = jnp.where(lane // 32 == k, pltpu.roll(s, (24 + 32 * k) % 128, 1), outer)
            SX[1, c, rows, :] = strip(inner, outer, pltpu.roll(PL[c], (4 - 8 * zt) % 128, 1),
                                      pltpu.roll(PR[c], (20 - 8 * zt) % 128, 1))

    strips = [remote(SX.at[1], SX.at[0], x_s.at[0], x_r.at[0], (mode_up, tile)),
              remote(SX.at[1], SX.at[2], x_s.at[1], x_r.at[1], (mode_dn, tile))]
    for copy in strips:
        copy.start()
    for copy in halo:
        copy.wait_recv()

    first_wave = wave_ref[0] + 64

    def evaluate(load, flows, rows, waves, base, target, step, blend, keep):
        for zt in range(4):
            span = slice(8 * zt, 8 * zt + 8)
            put = slice(8 + 8 * zt, 16 + 8 * zt)
            b, lo, up = load(span)
            local, above, below, right, left = terms(b, lo, up, flows(zt), rows, waves)
            for c in range(6):
                U[c, put, :] = above[c]
                if c < 4:
                    W[c, put, :] = below[c]
                partial = local[c] + pltpu.roll(right[c], 127, 1) + pltpu.roll(left[c], 1, 1)
                start = base[c, span, :]
                if blend:
                    start = 0.5 * start + 0.5 * b[c]
                target[c, span, :] = start + step * partial
        for c in range(6):
            low = U if c >= 4 else W
            for zt in range(4):
                span = slice(8 * zt, 8 * zt + 8)
                moved = U[c, 9 + 8 * zt:17 + 8 * zt, :] + low[c, 7 + 8 * zt:15 + 8 * zt, :]
                target[c, span, :] = keep(target[c, span, :] + step * moved)

    for e in range(4):
        cur, target = (S, T) if e % 2 == 0 else (T, S)
        shift = 0
        if e == 3:
            target, shift = out, 4
        step = TIME_STEP if e % 2 == 0 else 0.5 * TIME_STEP

        @pl.loop(e + 1, 11 - e)
        def _(slot, cur=cur, target=target, shift=shift, step=step, e=e):
            m = (((first_wave + (slot - 4) + 128) & 127) - 64).astype(F32)
            rows = [coef[0, i] for i in range(6)]

            def load(span):
                return [[cur[s, c, span, :] for c in range(6)] for s in (slot, slot - 1, slot + 1)]

            evaluate(load, lambda zt: [flow(f, zt) for f in range(9)], rows, wave_rows(m, rows),
                     S.at[slot], target.at[slot - shift], step, e % 2 == 1, lambda x: x)

    @pl.when(has_dn)
    def _():
        v_up.wait_recv()

    @pl.when(has_up)
    def _():
        v_dn.wait_recv()

    for f in range(9):
        for zt in range(4):
            i = 4 * (f % 4) + zt
            mine = flow(f, zt)
            x = strip(pltpu.roll(mine, 8, 1), pltpu.roll(mine, 24, 1), pltpu.roll(VL[f // 4], (4 - 8 * i) % 128, 1),
                      pltpu.roll(VR[f // 4], (20 - 8 * i) % 128, 1))
            x = jnp.where(lane < 32, x, pltpu.roll(x, 32, 1))
            VS[f, 8 * zt:8 * zt + 8, :] = jnp.where(lane < 64, x, pltpu.roll(x, 64, 1))

    for copy in strips:
        copy.wait_recv()
        copy.wait_send()

    inside = (cell >= 0) & (cell < n_tile * 128)
    for e in range(4):
        cur, target = (SX, ST) if e % 2 == 0 else (ST, SX)
        step = TIME_STEP if e % 2 == 0 else 0.5 * TIME_STEP

        @pl.loop(0 if e < 3 else 1, 3 if e < 3 else 2)
        def _(g, cur=cur, target=target, step=step, e=e):
            m = (((first_wave + (4 * g - 4 + lane // 32) + 128) & 127) - 64).astype(F32)
            rows = [coef[1, i] for i in range(6)]

            def load(span):
                b = [cur[g, c, span, :] for c in range(6)]
                lo = [pltpu.roll(jnp.where(lane >= 96, cur[(g + 2) % 3, c, span, :], b[c]), 32, 1) for c in range(6)]
                up = [pltpu.roll(jnp.where(lane < 32, cur[(g + 1) % 3, c, span, :], b[c]), 96, 1) for c in range(6)]
                return b, lo, up

            evaluate(load, lambda zt: [VS[f, 8 * zt:8 * zt + 8, :] for f in range(9)], rows, wave_rows(m, rows),
                     SX.at[g], target.at[g], step, e % 2 == 1, lambda x: jnp.where(inside, x, 0.0))

    @pl.loop(0, 6)
    def _(c):
        for zt in range(4):
            rows = slice(8 * zt, 8 * zt + 8)
            s = SX[1, c, rows, :]
            for k in range(4):
                edge = jnp.where(lane < 4, pltpu.roll(s, (120 - 32 * k) % 128, 1), out[k, c, rows, :])
                out[k, c, rows, :] = jnp.where(lane >= 124, pltpu.roll(s, (104 - 32 * k) % 128, 1), edge)

    for copy in spread + middle + gather + halo[:4]:
        copy.wait_send()

    @pl.when(top)
    def _():
        for copy in by_up + on_top:
            copy.wait_send()

    @pl.when(yc != 3)
    def _():
        for copy in halo[4::2]:
            copy.wait_send()

    @pl.when(low)
    def _():
        for copy in by_dn + on_low:
            copy.wait_send()

    @pl.when(yc != 0)
    def _():
        for copy in halo[5::2]:
            copy.wait_send()

    @pl.when(has_up)
    def _():
        to_up.wait_send()
        v_up.wait_send()

    @pl.when(has_dn)
    def _():
        to_dn.wait_send()
        v_dn.wait_send()


def body(n_tile, magnetic, velocity_stack, wavenumber, velocity_owner):
    vmem = pl.BlockSpec(memory_space=pltpu.VMEM)
    hbm = pl.BlockSpec(memory_space=pltpu.HBM)

    def keep(x):
        return pltpu.with_memory_space_constraint(x, pltpu.HBM)

    def dma(n):
        return pltpu.SemaphoreType.DMA((n,))

    def room(*shape):
        return pltpu.VMEM(shape, F32)

    return pl.pallas_call(
        functools.partial(kernel, n_tile),
        out_shape=jax.ShapeDtypeStruct((4, 6, 32, 128), F32),
        in_specs=[hbm, hbm, hbm, hbm],
        out_specs=vmem,
        scratch_shapes=[
            room(12, 6, 32, 128), room(12, 6, 32, 128), room(9, 32, 128), room(2, 5, 32, 128),
            room(7, 5, 8, 128), room(5, 8, 128), room(3, 5, 8, 128), room(2, 5, 32, 128),
            room(6, 48, 128), room(4, 48, 128), room(2, 6, 8, 128),
            room(6, 8, 128), room(6, 8, 128), room(6, 8, 128), room(3, 8, 128), room(3, 8, 128), room(3, 8, 128),
            room(9, 32, 128), room(3, 6, 32, 128), room(3, 6, 32, 128), room(2, 6, 32, 128), dma(2), dma(2), dma(2),
            pltpu.SMEM((4,), jnp.int32), pltpu.SMEM((1,), jnp.int32),
            dma(4), dma(7), dma(7), dma(3), dma(3), dma(7), dma(7), dma(8), dma(8),
            dma(2), dma(2), dma(2), dma(2), dma(2), dma(2),
        ],
        compiler_params=pltpu.CompilerParams(collective_id=0, has_side_effects=True, vmem_limit_bytes=32 << 20),
    )(keep(wavenumber), velocity_owner, keep(magnetic), keep(velocity_stack))


def solution(mesh):
    placed = (P("mode", None, None, "tile"), P("mode", None, None, "tile"), P("mode"), P())
    return jax.shard_map(
        functools.partial(body, mesh.shape["tile"]), mesh=mesh, in_specs=placed,
        out_specs=P("mode", None, None, "tile"), check_vma=False,
    )
```

```python
import functools

import jax
import jax.numpy as jnp
from jax import lax
from jax.experimental import pallas as pl
from jax.experimental.pallas import tpu as pltpu
from jax.sharding import PartitionSpec as P

MESH = pl.DeviceIdType.MESH
TIME_STEP = 0.2
INNER = 32.0
F32 = jnp.float32


def radius_rows(radius):
    before, after = radius - 1.0, radius + 1.0
    return [0.5 + 0.25 / before, 0.5 - 0.25 / after, 0.5 * radius / before, 0.5 * radius / after,
            1.0 / radius, 1.0 / (radius * radius)]


def wave_rows(m, rows):
    inv, inv2 = rows[4], rows[5]
    return m * inv, 2.0 + (0.5 * (m * m + 1.0)) * inv2, 2.0 + (0.5 * (m * m)) * inv2, m * inv2


def terms(b, lo, up, v, rows, waves):
    apm, amp, flp, flm = rows[:4]
    w, dec, decz, cpl = waves
    sums = [lo[c] + up[c] for c in range(6)]
    swap = [None] * 6
    for k in range(3):
        swap[2 * k] = up[2 * k + 1] - lo[2 * k + 1]
        swap[2 * k + 1] = lo[2 * k] - up[2 * k]
    e = []
    for k in range(3):
        s, t = (k + 1) % 3, (k + 2) % 3
        for q in range(2):
            i, j = 2 * t + q, 2 * s + q
            e.append((v[s] * b[i] - v[t] * b[j]) + (v[3 + 2 * s] * sums[i] + v[4 + 2 * s] * swap[i])
                     - (v[3 + 2 * t] * sums[j] + v[4 + 2 * t] * swap[j]))
    local = [
        cpl * b[3] - w * e[5] - dec * b[0],
        w * e[4] - cpl * b[2] - dec * b[1],
        -(dec * b[2] + cpl * b[1]),
        cpl * b[0] - dec * b[3],
        w * e[1] - decz * b[4],
        -(w * e[0] + decz * b[5]),
    ]
    half_b = [0.5 * b[c] for c in range(6)]
    half_e = [0.5 * e[c] for c in range(6)]
    above, below, right, left = [], [], [], []
    for c in range(6):
        if c < 2:
            above.append(half_b[c] - half_e[2 + c])
            below.append(half_b[c] + half_e[2 + c])
        elif c < 4:
            above.append(half_b[c] + half_e[c - 2])
            below.append(half_b[c] - half_e[c - 2])
        else:
            above.append(half_b[c])
        right.append(apm * b[c])
        left.append(amp * b[c])
        if c in (2, 3):
            right[c] = right[c] - half_e[c + 2]
            left[c] = left[c] + half_e[c + 2]
        elif c >= 4:
            right[c] = right[c] + flp * e[c - 2]
            left[c] = left[c] - flm * e[c - 2]
    return local, above, below, right, left


def kernel(n_tile, wave_hbm, owner_hbm, mag, vel, out, S, T, Vin, M, R1, Q, R2, V, U, W, coef, P0, PL, PR, PV, VL, VR,
           VS, SX, ST, RB, r_s, r_r, f_s, wave_ref, owner_ref, lsem, y_s, y_r, z_s, z_r, g_s, g_r, m_s, m_r, t_s, t_r, v_s, v_r, x_s, x_r):
    mode = lax.axis_index("mode")
    tile = lax.axis_index("tile")
    zc = mode // 4
    yc = mode % 4
    par = zc % 2
    zg = zc // 2

    load_w = pltpu.make_async_copy(wave_hbm, wave_ref, lsem.at[2])
    load_w.start()
    load_o = pltpu.make_async_copy(owner_hbm, owner_ref, lsem.at[3])
    load_o.start()
    load_v = pltpu.make_async_copy(vel.at[0], Vin, lsem.at[0])
    load_v.start()
    load_s = pltpu.make_async_copy(mag, S.at[pl.ds(4, 4)], lsem.at[1])
    load_s.start()

    mode_up = (mode + 1) % 32
    mode_dn = (mode + 31) % 32
    mode_next = (mode + 4) % 32
    mode_prev = (mode + 28) % 32
    near = []
    for dp in range(2):
        for dy in range(4):
            if dp + dy:
                q, y = (par + dp) % 2, (yc + dy) % 4
                near.append((q, y, (2 * zg + q) * 4 + y))
    across = [(2 * ((zg + d) % 4) + par) * 4 + yc for d in (1, 2, 3)]
    has_up, has_dn = tile < n_tile - 1, tile > 0
    tile_up = (tile + 1) % n_tile
    tile_dn = (tile + n_tile - 1) % n_tile

    barrier = pltpu.get_barrier_semaphore()
    everyone = [(m, tile) for _, _, m in near] + [(m, tile) for m in across] + [(mode_up, tile), (mode_dn, tile), (mode, tile_up), (mode, tile_dn)]
    everyone += [(mode_next, tile), (mode_prev, tile)]
    for where in everyone:
        pl.semaphore_signal(barrier, inc=1, device_id=where, device_id_type=MESH)
    lane = lax.broadcasted_iota(jnp.int32, (8, 128), 1)
    for i, row in enumerate(radius_rows(INNER + (tile * 128 + lane).astype(F32) + 0.5)):
        coef[0, i] = row
    place = lane % 32
    cell = jnp.where(place < 16, place - 8, place + 104) + tile * 128
    for i, row in enumerate(radius_rows(INNER + cell.astype(F32) + 0.5)):
        coef[1, i] = row
    zero = jnp.zeros((8, 128), F32)
    for c in range(6):
        for edge in (0, 40):
            U[c, edge:edge + 8, :] = zero
            if c < 4:
                W[c, edge:edge + 8, :] = zero

    @pl.when(tile == 0)
    def _():
        PL[...] = jnp.zeros_like(PL)
        VL[...] = jnp.zeros_like(VL)

    @pl.when(tile == n_tile - 1)
    def _():
        PR[...] = jnp.zeros_like(PR)
        VR[...] = jnp.zeros_like(VR)

    load_o.wait()
    load_w.wait()
    load_v.wait()
    mine = owner_ref[0] == mode
    M[0] = jnp.where(mine, Vin[0:5], 0.0)
    M[1] = jnp.where(mine, Vin[4:9], 0.0)
    pl.semaphore_wait(barrier, len(everyone))
    def remote(source, to, send, recv, where):
        return pltpu.make_async_remote_copy(source, to, send, recv, device_id=where, device_id_type=MESH)

    own = pl.ds(pl.multiple_of(yc * 8, 8), 8)
    spread, gather = [], []
    for i, (q, y, m) in enumerate(near):
        rows = pl.ds(pl.multiple_of(y * 8, 8), 8)
        spread.append(remote(M.at[q, :, rows, :], R1.at[i], y_s.at[i], y_r.at[i], (m, tile)))
        gather.append(remote(V.at[par, :, own, :], V.at[par, :, own, :], g_s.at[i], g_r.at[i], (m, tile)))
    for copy in spread:
        copy.start()

    halo = []
    for i in range(4):
        halo.append(remote(mag.at[3 - i], S.at[3 - i], m_s.at[2 * i], m_r.at[2 * i], (mode_up, tile)))
        halo.append(remote(mag.at[i], S.at[8 + i], m_s.at[2 * i + 1], m_r.at[2 * i + 1], (mode_dn, tile)))

    for copy in halo[:4]:
        copy.start()
    by_up, by_dn, on_top, on_low = [], [], [], []
    for j in range(2):
        i = 2 + j
        by_up.append(remote(mag.at[3 - i], RB.at[j], r_s.at[j], r_r.at[j], ((mode + 29) % 32, tile)))
        by_dn.append(remote(mag.at[i], RB.at[j], r_s.at[j], r_r.at[j], ((mode + 3) % 32, tile)))
        on_top.append(remote(RB.at[j], S.at[8 + i], f_s.at[j], m_r.at[2 * i + 1], (mode_prev, tile)))
        on_low.append(remote(RB.at[j], S.at[3 - i], f_s.at[j], m_r.at[2 * i], (mode_next, tile)))
    top, low = yc == 3, yc == 0

    @pl.when(top)
    def _():
        for copy in by_up:
            copy.start()

    @pl.when(yc != 3)
    def _():
        for copy in halo[4::2]:
            copy.start()

    @pl.when(low)
    def _():
        for copy in by_dn:
            copy.start()

    @pl.when(yc != 0)
    def _():
        for copy in halo[5::2]:
            copy.start()


    load_s.wait()
    eighth = place // 8

    @pl.loop(0, 6)
    def _(c):
        packed = zero
        for k in range(4):
            for zt in range(4):
                moved = pltpu.roll(S[4 + k, c, 8 * zt:8 * zt + 8, :], (4 + 32 * k + 8 * zt) % 128, 1)
                packed = jnp.where((eighth == zt) & (lane // 32 == k), moved, packed)
        P0[c] = packed

    to_up = remote(P0, PL, t_s.at[0], t_r.at[0], (mode, tile_up))
    to_dn = remote(P0, PR, t_s.at[1], t_r.at[1], (mode, tile_dn))
    v_up = remote(PV, VL, v_s.at[0], v_r.at[0], (mode, tile_up))
    v_dn = remote(PV, VR, v_s.at[1], v_r.at[1], (mode, tile_dn))

    @pl.when(has_up)
    def _():
        to_up.start()

    @pl.when(has_dn)
    def _():
        to_dn.start()

    total = M[par, :, own, :]
    for i in range(7):
        spread[i].wait_recv()
        total = total + R1[i]
    Q[...] = total
    middle = [remote(Q, R2.at[i], z_s.at[i], z_r.at[i], (across[i], tile)) for i in range(3)]
    for copy in middle:
        copy.start()

    @pl.when(top)
    def _():
        for j in range(2):
            by_up[j].wait_recv()
            on_top[j].start()

    @pl.when(low)
    def _():
        for j in range(2):
            by_dn[j].wait_recv()
            on_low[j].start()


    total = Q[...]
    for i in range(3):
        middle[i].wait_recv()
        total = total + R2[i]
    V[par, :, own, :] = total
    for copy in gather:
        copy.start()

    @pl.when(has_dn)
    def _():
        to_up.wait_recv()

    @pl.when(has_up)
    def _():
        to_dn.wait_recv()

    def strip(inner, outer, from_left, from_right):
        got = jnp.where((place >= 8) & (place < 16), inner, jnp.where((place >= 16) & (place < 24), outer, 0.0))
        got = jnp.where((place >= 4) & (place < 8), from_left, got)
        return jnp.where((place >= 24) & (place < 28), from_right, got)

    @pl.loop(0, 6)
    def _(c):
        for zt in range(4):
            rows = slice(8 * zt, 8 * zt + 8)
            inner, outer = zero, zero
            for k in range(4):
                s = S[4 + k, c, rows, :]
                inner = jnp.where(lane // 32 == k, pltpu.roll(s, (8 + 32 * k) % 128, 1), inner)
                outer = jnp.where(lane // 32 == k, pltpu.roll(s, (24 + 32 * k) % 128, 1), outer)
            SX[1, c, rows, :] = strip(inner, outer, pltpu.roll(PL[c], (4 - 8 * zt) % 128, 1),
                                      pltpu.roll(PR[c], (20 - 8 * zt) % 128, 1))

    strips = [remote(SX.at[1], SX.at[0], x_s.at[0], x_r.at[0], (mode_up, tile)),
              remote(SX.at[1], SX.at[2], x_s.at[1], x_r.at[1], (mode_dn, tile))]
    for copy in strips:
        copy.start()
    for copy in gather:
        copy.wait_recv()

    def flow(f, zt):
        return V[f // 4 if f < 8 else 1, f % 4 if f < 8 else 4, 8 * zt:8 * zt + 8, :]

    for block in range(3):
        packed = zero
        for f in range(4 * block, min(9, 4 * block + 4)):
            for zt in range(4):
                i = 4 * (f % 4) + zt
                packed = jnp.where(lane // 8 == i, pltpu.roll(flow(f, zt), (4 + 8 * i) % 128, 1), packed)
        PV[block] = packed

    @pl.when(has_up)
    def _():
        v_up.start()

    @pl.when(has_dn)
    def _():
        v_dn.start()

    for copy in halo:
        copy.wait_recv()

    first_wave = wave_ref[0] + 64

    def evaluate(load, flows, rows, waves, base, target, step, blend, keep):
        for zt in range(4):
            span = slice(8 * zt, 8 * zt + 8)
            put = slice(8 + 8 * zt, 16 + 8 * zt)
            b, lo, up = load(span)
            local, above, below, right, left = terms(b, lo, up, flows(zt), rows, waves)
            for c in range(6):
                U[c, put, :] = above[c]
                if c < 4:
                    W[c, put, :] = below[c]
                partial = local[c] + pltpu.roll(right[c], 127, 1) + pltpu.roll(left[c], 1, 1)
                start = base[c, span, :]
                if blend:
                    start = 0.5 * start + 0.5 * b[c]
                target[c, span, :] = start + step * partial
        for c in range(6):
            low = U if c >= 4 else W
            for zt in range(4):
                span = slice(8 * zt, 8 * zt + 8)
                moved = U[c, 9 + 8 * zt:17 + 8 * zt, :] + low[c, 7 + 8 * zt:15 + 8 * zt, :]
                target[c, span, :] = keep(target[c, span, :] + step * moved)

    for e in range(4):
        cur, target = (S, T) if e % 2 == 0 else (T, S)
        shift = 0
        if e == 3:
            target, shift = out, 4
        step = TIME_STEP if e % 2 == 0 else 0.5 * TIME_STEP

        @pl.loop(e + 1, 11 - e)
        def _(slot, cur=cur, target=target, shift=shift, step=step, e=e):
            m = (((first_wave + (slot - 4) + 128) & 127) - 64).astype(F32)
            rows = [coef[0, i] for i in range(6)]

            def load(span):
                return [[cur[s, c, span, :] for c in range(6)] for s in (slot, slot - 1, slot + 1)]

            evaluate(load, lambda zt: [flow(f, zt) for f in range(9)], rows, wave_rows(m, rows),
                     S.at[slot], target.at[slot - shift], step, e % 2 == 1, lambda x: x)

    @pl.when(has_dn)
    def _():
        v_up.wait_recv()

    @pl.when(has_up)
    def _():
        v_dn.wait_recv()

    for f in range(9):
        for zt in range(4):
            i = 4 * (f % 4) + zt
            mine = flow(f, zt)
            x = strip(pltpu.roll(mine, 8, 1), pltpu.roll(mine, 24, 1), pltpu.roll(VL[f // 4], (4 - 8 * i) % 128, 1),
                      pltpu.roll(VR[f // 4], (20 - 8 * i) % 128, 1))
            x = jnp.where(lane < 32, x, pltpu.roll(x, 32, 1))
            VS[f, 8 * zt:8 * zt + 8, :] = jnp.where(lane < 64, x, pltpu.roll(x, 64, 1))

    for copy in strips:
        copy.wait_recv()
        copy.wait_send()

    inside = (cell >= 0) & (cell < n_tile * 128)
    for e in range(4):
        cur, target = (SX, ST) if e % 2 == 0 else (ST, SX)
        step = TIME_STEP if e % 2 == 0 else 0.5 * TIME_STEP

        @pl.loop(0 if e < 3 else 1, 3 if e < 3 else 2)
        def _(g, cur=cur, target=target, step=step, e=e):
            m = (((first_wave + (4 * g - 4 + lane // 32) + 128) & 127) - 64).astype(F32)
            rows = [coef[1, i] for i in range(6)]

            def load(span):
                b = [cur[g, c, span, :] for c in range(6)]
                lo = [pltpu.roll(jnp.where(lane >= 96, cur[(g + 2) % 3, c, span, :], b[c]), 32, 1) for c in range(6)]
                up = [pltpu.roll(jnp.where(lane < 32, cur[(g + 1) % 3, c, span, :], b[c]), 96, 1) for c in range(6)]
                return b, lo, up

            evaluate(load, lambda zt: [VS[f, 8 * zt:8 * zt + 8, :] for f in range(9)], rows, wave_rows(m, rows),
                     SX.at[g], target.at[g], step, e % 2 == 1, lambda x: jnp.where(inside, x, 0.0))

    @pl.loop(0, 6)
    def _(c):
        for zt in range(4):
            rows = slice(8 * zt, 8 * zt + 8)
            s = SX[1, c, rows, :]
            for k in range(4):
                edge = jnp.where(lane < 4, pltpu.roll(s, (120 - 32 * k) % 128, 1), out[k, c, rows, :])
                out[k, c, rows, :] = jnp.where(lane >= 124, pltpu.roll(s, (104 - 32 * k) % 128, 1), edge)

    for copy in spread + middle + gather + halo[:4]:
        copy.wait_send()

    @pl.when(top)
    def _():
        for copy in by_up + on_top:
            copy.wait_send()

    @pl.when(yc != 3)
    def _():
        for copy in halo[4::2]:
            copy.wait_send()

    @pl.when(low)
    def _():
        for copy in by_dn + on_low:
            copy.wait_send()

    @pl.when(yc != 0)
    def _():
        for copy in halo[5::2]:
            copy.wait_send()

    @pl.when(has_up)
    def _():
        to_up.wait_send()
        v_up.wait_send()

    @pl.when(has_dn)
    def _():
        to_dn.wait_send()
        v_dn.wait_send()


def body(n_tile, magnetic, velocity_stack, wavenumber, velocity_owner):
    vmem = pl.BlockSpec(memory_space=pltpu.VMEM)
    hbm = pl.BlockSpec(memory_space=pltpu.HBM)

    def keep(x):
        return pltpu.with_memory_space_constraint(x, pltpu.HBM)

    def dma(n):
        return pltpu.SemaphoreType.DMA((n,))

    def room(*shape):
        return pltpu.VMEM(shape, F32)

    return pl.pallas_call(
        functools.partial(kernel, n_tile),
        out_shape=jax.ShapeDtypeStruct((4, 6, 32, 128), F32),
        in_specs=[hbm, hbm, hbm, hbm],
        out_specs=vmem,
        scratch_shapes=[
            room(12, 6, 32, 128), room(12, 6, 32, 128), room(9, 32, 128), room(2, 5, 32, 128),
            room(7, 5, 8, 128), room(5, 8, 128), room(3, 5, 8, 128), room(2, 5, 32, 128),
            room(6, 48, 128), room(4, 48, 128), room(2, 6, 8, 128),
            room(6, 8, 128), room(6, 8, 128), room(6, 8, 128), room(3, 8, 128), room(3, 8, 128), room(3, 8, 128),
            room(9, 32, 128), room(3, 6, 32, 128), room(3, 6, 32, 128), room(2, 6, 32, 128), dma(2), dma(2), dma(2),
            pltpu.SMEM((4,), jnp.int32), pltpu.SMEM((1,), jnp.int32),
            dma(4), dma(7), dma(7), dma(3), dma(3), dma(7), dma(7), dma(8), dma(8),
            dma(2), dma(2), dma(2), dma(2), dma(2), dma(2),
        ],
        compiler_params=pltpu.CompilerParams(collective_id=0, has_side_effects=True, vmem_limit_bytes=32 << 20),
    )(keep(wavenumber), velocity_owner, keep(magnetic), keep(velocity_stack))


def solution(mesh):
    placed = (P("mode", None, None, "tile"), P("mode", None, None, "tile"), P("mode"), P())
    return jax.shard_map(
        functools.partial(body, mesh.shape["tile"]), mesh=mesh, in_specs=placed,
        out_specs=P("mode", None, None, "tile"), check_vma=False,
    )
```
